512 devices in a mesh: date: 4 (over y_hi, core), space: 128 (over z, y_lo, x).
Axes of the slice: x: 4, y: 8 (y_hi: 2, y_lo: 4; y = y_hi * 4 + y_lo), z: 8, core: 2. Of those that a mesh axis runs over, the one named last changes fastest.
Arguments:
- stack: float32 [2, 28, 1024, 1024], P(None, 'date', 'space'), may hold values from -6 to 6
Outputs:
- coherence: float32 [14, 28, 1024, 1024], P(None, None, 'space', 'date')
The draws below stay inside these ranges and needn't reach their ends.
All inputs are finite; a program needn't handle non-finite values.
Results may differ from the reference program's by a relative error of at most 0.000068.
Values sent between devices are 32-bit elements; how exact they have to be, the bound alone decides.
No kernel may reach another device: no remote copies, remote signals or barrier semaphores. Data moves between devices by JAX's collectives and lax.ppermute only.
A program may use at most 64 MiB of HBM per device.

```python
import jax
import jax.numpy as jnp
from jax import lax

DATES = 28
LAGS = 14
WIN_AZ = 11
WIN_RG = 23
AZ = 1024
RG = 1024


def shard_levels(stream_key, dims, cuts, smallest, top_value):
    def one(axis_at, shards_of):
        heights = jax.random.uniform(jax.random.fold_in(jax.random.fold_in(stream_key, 6), axis_at), (shards_of,), jnp.float32, smallest / len(cuts), top_value / len(cuts))
        return jnp.repeat(jnp.exp(heights), dims[axis_at] // shards_of).reshape((-1,) + (1,) * (len(dims) - axis_at - 1))

    loudness = one(*cuts[0])
    for cut in cuts[1:]:
        loudness = loudness * one(*cut)
    return loudness


def bell_draw(key, dims, deviation, most, pieces=(), kind=jnp.bfloat16):
    entries = jax.random.normal(key, dims, jnp.float32) * deviation
    if len(pieces) > 0:
        entries = shard_levels(key, dims, pieces, -0.22, 0.18) * entries
    return jnp.clip(entries, min=-most, max=most).astype(kind)


def setup_inputs(seed: int = 0) -> dict:
    key_of = jax.random.split(jax.random.key(seed), 2)
    return {
        "stack": bell_draw(key_of[0], (2, DATES, AZ, RG), 1.0, 6.0, ((1, 4), (2, 128)), jnp.float32),
    }


def boxcar(values):
    half_az = WIN_AZ // 2
    half_rg = WIN_RG // 2
    rows = values.shape[-2]
    cols = values.shape[-1]
    padded = jnp.pad(values, ((0, 0), (half_az, half_az), (half_rg, half_rg)))
    summed = padded[:, 0:rows, :]
    for offset in range(1, WIN_AZ):
        summed = summed + padded[:, offset:offset + rows, :]
    total = summed[:, :, 0:cols]
    for offset in range(1, WIN_RG):
        total = total + summed[:, :, offset:offset + cols]
    return total

def reference(stack):
    real_part = stack[0]
    imag_part = stack[1]
    power = boxcar(real_part * real_part + imag_part * imag_part)

    def one_lag(lag):
        shift = lag + 1
        real_other = jnp.roll(real_part, -shift, axis=0)
        imag_other = jnp.roll(imag_part, -shift, axis=0)
        power_other = jnp.roll(power, -shift, axis=0)
        cross_re = boxcar(real_part * real_other + imag_part * imag_other)
        cross_im = boxcar(imag_part * real_other - real_part * imag_other)
        return jnp.sqrt(cross_re * cross_re + cross_im * cross_im) / jnp.sqrt(power * power_other)
    return lax.map(one_lag, jnp.arange(LAGS, dtype=jnp.int32))
```

```python
import functools

import jax
import jax.numpy as jnp
import numpy as np
from jax import lax
from jax.experimental import pallas as pl
from jax.experimental.pallas import tpu as pltpu
from jax.sharding import PartitionSpec as P

WIN_AZ = 11
WIN_RG = 23
HALF_AZ = WIN_AZ // 2
HALF_RG = WIN_RG // 2
DATES = 28
LAGS = 14
GROUPS = 4
PER = 7
ROWS = 8
TALL = ROWS + 2 * HALF_AZ
BLOCK = 32
TILES = GROUPS * 2
LANES = 128
ROWLEN = 2 * 2 * 8
TINY = float(np.finfo(np.float32).tiny)
PASSES = [(0, m) for m in (1, 2, 3)] + [(1, m) for m in range(7)] + [(2, m) for m in range(4)]


def lag_table():
    where = {}
    for t, (delta, m) in enumerate(PASSES):
        for q in range(GROUPS):
            for u in range(PER):
                i, j = 7 * q + u, 7 * ((q + delta) % 4) + (u + m) % 7
                start = (t * 4 + q) * 128 + u
                where[(i, j)] = start
                where.setdefault((j, i), start)
    return np.array(
        [[where[(i, (i + k + 1) % DATES)] for i in range(DATES)] for k in range(LAGS)], np.int32
    ).reshape(-1)


def lane_iota(shape):
    return lax.broadcasted_iota(jnp.int32, shape, len(shape) - 1)


def pack_kernel(x_ref, o_ref):
    lane = lane_iota((8, LANES))
    sub = lax.broadcasted_iota(jnp.int32, (8, LANES), 0)
    own = (lane // BLOCK) == (sub % 4)
    for row in range(ROWS):
        for part in range(2):
            tiles = [
                x_ref[pl.ds(part * 448 + tile * 8 + row, PER, stride=64), :] for tile in range(TILES)
            ]
            zero = jnp.zeros((PER, LANES), jnp.float32)
            for q in range(GROUPS):
                base = (row * 2 + part) * 16
                left = tiles[2 * q - 1] if q > 0 else zero
                right = tiles[2 * q + 2] if q < 3 else zero
                near = jnp.where(lane[:PER] >= LANES - HALF_RG, left, right)
                near = jnp.concatenate([near, jnp.zeros((1, LANES), jnp.float32)], axis=0)
                turned = jnp.zeros((8, LANES), jnp.float32)
                for v in range(4):
                    moved = pltpu.roll(near, HALF_RG + BLOCK * v, 1)
                    turned = jnp.where(own & (sub % 4 == v), moved, turned)
                for half in range(2):
                    o_ref[q, pl.ds(base + half * 8, PER), :] = tiles[2 * q + half]
                    line = jnp.sum(turned[4 * half : 4 * half + 4], axis=0, keepdims=True)
                    o_ref[q, pl.ds(base + half * 8 + 7, 1), :] = line


def sum_rows(row_of):
    core = row_of(7) + row_of(8) + row_of(9) + row_of(10)
    down = [None] * 8
    down[7] = core
    for r in range(6, -1, -1):
        down[r] = down[r + 1] + row_of(r)
    sums = [down[0]]
    up = None
    for r in range(1, 8):
        row = row_of(r + 10)
        up = row if up is None else up + row
        sums.append(down[r] + up)
    return sums


def add(a, b):
    return a[0] + b[0], a[1] + b[1]


class Two(tuple):
    def __add__(self, other):
        return Two((self[0] + other[0], self[1] + other[1]))


def split(a, b):
    both = jnp.concatenate([a, b], axis=0)
    high = both.astype(jnp.bfloat16)
    low = (both - high.astype(jnp.float32)).astype(jnp.bfloat16)
    return high, low


def main_kernel(table, mid_ref, top_ref, bot_ref, o_ref, dates, halos, band, lhs, weights, res):
    lane = lane_iota((8, LANES))
    sub = lax.broadcasted_iota(jnp.int32, (8, LANES), 0)

    for block in range(6):
        src = lax.broadcasted_iota(jnp.int32, (LANES, 256), 0)
        dst = lane_iota((LANES, 256))
        if block < 4:
            col = src + (block % 2) * LANES
            hit = jnp.abs(col - dst) <= HALF_RG
        else:
            x = src % BLOCK
            col = jnp.where(x < HALF_RG, x - HALF_RG, x - HALF_RG + 256)
            hit = (jnp.abs(col - dst) <= HALF_RG) & (x < 2 * HALF_RG)
        band[block * LANES : (block + 1) * LANES, :] = jnp.where(hit, 1.0, 0.0).astype(jnp.bfloat16)

    def prepare(ref, rows, first):
        def one(row, carry):
            for part in range(2):
                base = (row * 2 + part) * 16
                lines = [[None, None] for _ in range(GROUPS)]
                for half in range(2):
                    for g in range(GROUPS):
                        start = pl.multiple_of(base + half * 8, 8)
                        tile = ref[g, pl.ds(start, 8), :]
                        slot = ((part * 4 + g) * 2 + half) * TALL + first + row
                        dates[slot, 0:8, :] = tile
                        dates[slot, 7:14, :] = tile[0:PER]
                        lines[g][half] = jnp.broadcast_to(tile[7:8], (8, LANES))
                lines = [jnp.where(sub < 4, low, high) for low, high in lines]
                halo = jnp.zeros((8, LANES), jnp.float32)
                for e in range(4):
                    moved = lines[(3 + e) % 4]
                    for v in range(3):
                        moved = jnp.where(sub % 4 == v, lines[(v + e) % 4], moved)
                    moved = pltpu.roll(moved, BLOCK * e, 1) if e else moved
                    halo = jnp.where(lane // BLOCK == (sub + e) % 4, moved, halo)
                for delta in range(3):
                    turned = pltpu.roll(halo, (LANES - BLOCK * delta) % LANES, 1) if delta else halo
                    slot = (delta * 2 + part) * TALL + first + row
                    halos[slot, 0:8, :] = turned
                    halos[slot, 7:14, :] = turned[0:PER]
            return carry

        lax.fori_loop(0, rows, one, 0)

    prepare(top_ref, HALF_AZ, 0)
    prepare(mid_ref, ROWS, HALF_AZ)
    prepare(bot_ref, HALF_AZ, HALF_AZ + ROWS)

    def put(rows, tile, sums):
        for r in range(0, 8, 2):
            high, low = split(sums[r], sums[r + 1])
            lhs[rows + r * 8 : rows + r * 8 + 16, tile * LANES : (tile + 1) * LANES] = high
            lhs[rows + r * 8 : rows + r * 8 + 16, (tile + 2) * LANES : (tile + 3) * LANES] = low

    def put_halo(first, step, sums):
        blocks = lane_iota((16, LANES)) // BLOCK
        keep = [jnp.where(blocks == q, 1.0, 0.0).astype(jnp.bfloat16) for q in range(GROUPS)]
        for r in range(0, 8, 2):
            high, low = split(sums[r], sums[r + 1])
            for q in range(GROUPS):
                rows = first + q * step + r * 8
                lhs[rows : rows + 16, 4 * LANES : 5 * LANES] = high * keep[q]
                lhs[rows : rows + 16, 5 * LANES : 6 * LANES] = low * keep[q]

    def energy(ref, re_slot, im_slot):
        def row_of(row):
            re = ref[re_slot + row, 0:8, :]
            im = ref[im_slot + row, 0:8, :]
            return re * re + im * im

        return sum_rows(row_of)

    for g in range(GROUPS):
        for half in range(2):
            put(g * 64, half, energy(dates, (g * 2 + half) * TALL, ((4 + g) * 2 + half) * TALL))
    put_halo(0, 64, energy(halos, 0, TALL))
    power = jnp.dot(lhs[0:256, :], band[...], preferred_element_type=jnp.float32)
    root = lax.rsqrt(power)
    for g in range(GROUPS):
        for r in range(8):
            for half in range(2):
                tile = root[g * 64 + r * 8 : g * 64 + r * 8 + 8, half * LANES : (half + 1) * LANES]
                weights[(g * 8 + r) * 2 + half, 0:8, :] = tile
                weights[(g * 8 + r) * 2 + half, 7:14, :] = tile[0:PER]

    def cross(ref, i_re, i_im, j_re, j_im, m):
        def row_of(row):
            are = ref[i_re + row, 0:8, :]
            aim = ref[i_im + row, 0:8, :]
            bre = ref[j_re + row, pl.ds(m, 8), :]
            bim = ref[j_im + row, pl.ds(m, 8), :]
            return Two((are * bre + aim * bim, aim * bre - are * bim))

        return sum_rows(row_of)

    def one_pass(t, carry):
        delta = jnp.where(t < 3, 0, jnp.where(t < 10, 1, 2))
        m = jnp.where(t < 3, t + 1, jnp.where(t < 10, t - 3, t - 10))
        for q in range(GROUPS):
            other = (q + delta) % 4
            for half in range(2):
                sums = cross(
                    dates,
                    (q * 2 + half) * TALL,
                    ((4 + q) * 2 + half) * TALL,
                    (other * 2 + half) * TALL,
                    ((4 + other) * 2 + half) * TALL,
                    m,
                )
                put(q * 128, half, [s[0] for s in sums])
                put(q * 128 + 64, half, [s[1] for s in sums])
        sums = cross(halos, 0, TALL, delta * 2 * TALL, (delta * 2 + 1) * TALL, m)
        put_halo(0, 128, [s[0] for s in sums])
        put_halo(64, 128, [s[1] for s in sums])
        boxed = jnp.dot(lhs[...], band[...], preferred_element_type=jnp.float32)
        for q in range(GROUPS):
            other = (q + delta) % 4
            for r in range(8):
                for half in range(2):
                    cols = slice(half * LANES, (half + 1) * LANES)
                    re = boxed[q * 128 + r * 8 : q * 128 + r * 8 + 8, cols]
                    im = boxed[q * 128 + 64 + r * 8 : q * 128 + 64 + r * 8 + 8, cols]
                    square = re * re + im * im
                    size = square * lax.rsqrt(jnp.maximum(square, TINY))
                    wi = weights[(q * 8 + r) * 2 + half, 0:8, :]
                    wj = weights[(other * 8 + r) * 2 + half, pl.ds(m, 8), :]
                    start = pl.multiple_of((t * 4 + q) * 128 + r * 16 + half * 8, 8)
                    res[pl.ds(start, 8), :] = size * wi * wj
        return carry

    lax.fori_loop(0, len(PASSES), one_pass, 0)

    def emit(k, carry):
        for i in range(DATES):
            start = table[k * DATES + i]
            for half in range(2):
                target = pl.multiple_of(((k * DATES + i) * 2 + half) * 8, 8)
                o_ref[pl.ds(target, 8), :] = res[pl.ds(start + half * 8, 8, stride=16), :]
        return carry

    lax.fori_loop(0, LAGS, emit, 0)


VMEM = pl.BlockSpec(memory_space=pltpu.VMEM)


def pack(stack):
    flat = stack.reshape(2, PER, ROWS, TILES, LANES).transpose(0, 1, 3, 2, 4).reshape(-1, LANES)
    return pl.pallas_call(
        pack_kernel,
        out_shape=jax.ShapeDtypeStruct((GROUPS, ROWS * ROWLEN, LANES), jnp.float32),
        in_specs=[VMEM],
        out_specs=VMEM,
    )(flat)


def coherence(mid, top, bottom):
    out = pl.pallas_call(
        main_kernel,
        out_shape=jax.ShapeDtypeStruct((LAGS * DATES * 2 * 8, LANES), jnp.float32),
        in_specs=[pl.BlockSpec(memory_space=pltpu.SMEM), VMEM, VMEM, VMEM],
        out_specs=VMEM,
        scratch_shapes=[
            pltpu.VMEM((2 * 4 * 2 * TALL, 16, LANES), jnp.float32),
            pltpu.VMEM((3 * 2 * TALL, 16, LANES), jnp.float32),
            pltpu.VMEM((6 * LANES, 256), jnp.bfloat16),
            pltpu.VMEM((512, 6 * LANES), jnp.bfloat16),
            pltpu.VMEM((4 * 8 * 2, 16, LANES), jnp.float32),
            pltpu.VMEM((len(PASSES) * 4 * 128, LANES), jnp.float32),
        ],
        compiler_params=pltpu.CompilerParams(vmem_limit_bytes=40 * 1024 * 1024),
    )(jnp.asarray(lag_table()), mid, top, bottom)
    return (
        out.reshape(LAGS, DATES, 2, ROWS, LANES)
        .transpose(0, 1, 3, 2, 4)
        .reshape(LAGS, DATES, ROWS, 2 * LANES)
    )


def body(stack):
    sent = pack(stack)
    mid = lax.all_to_all(sent, "date", 0, 0, tiled=True)
    peers = lax.axis_size("space")
    up = [(i, i + 1) for i in range(peers - 1)]
    down = [(i + 1, i) for i in range(peers - 1)]
    top = lax.ppermute(mid[:, (ROWS - HALF_AZ) * ROWLEN :], "space", up)
    bottom = lax.ppermute(mid[:, : HALF_AZ * ROWLEN], "space", down)
    return coherence(mid, top, bottom)


def solution(mesh):
    in_specs = (P(None, "date", "space", None),)
    out_specs = P(None, None, "space", "date")
    return jax.shard_map(body, mesh=mesh, in_specs=in_specs, out_specs=out_specs, check_vma=False)
```

```python
import jax
import jax.numpy as jnp
import numpy as np
from jax import lax
from jax.experimental import pallas as pl
from jax.experimental.pallas import tpu as pltpu
from jax.sharding import PartitionSpec as P

WIN_AZ = 11
WIN_RG = 23
HALF_AZ = WIN_AZ // 2
HALF_RG = WIN_RG // 2
DATES = 28
LAGS = 14
GROUPS = 4
PER = 7
ROWS = 8
TALL = ROWS + 2 * HALF_AZ
BLOCK = 32
TILES = GROUPS * 2
LANES = 128
ROWLEN = 2 * 2 * 8
MIDLEN = ROWS * ROWLEN
HALOLEN = HALF_AZ * ROWLEN
TINY = float(np.finfo(np.float32).tiny)

INNER = [(True, m) for m in (1, 2, 3)] + [(False, m) for m in range(4)] + [(False, 3)]
OUTER = [(0, 2), (1, 3), (2, 1), (3, 0)]
NEAR_ROWS = len(INNER) * 2 * 128
RES_ROWS = 2 * NEAR_ROWS + 7 * 4 * 128


def lag_tables():
    out = []
    for a in range(GROUPS):
        where = {}

        def note(start, pi, pj, m):
            for u in range(PER):
                i, j = 7 * (pi ^ a) + u, 7 * (pj ^ a) + (u + m) % 7
                where.setdefault((i, j), start + u)
                where.setdefault((j, i), start + u)

        for far in range(2):
            for n, (same, m) in enumerate(INNER):
                for q in range(2):
                    p = 2 * far + q
                    note(far * NEAR_ROWS + (n * 2 + q) * 128, p, p if same else p ^ 1, m)
        for m in range(7):
            for q, (pi, pj) in enumerate(OUTER):
                note(2 * NEAR_ROWS + (m * 4 + q) * 128, pi, pj, m)
        out += [where[(i, (i + k + 1) % DATES)] for k in range(LAGS) for i in range(DATES)]
    return np.array(out, np.int32)


def lanes_of(shape):
    return lax.broadcasted_iota(jnp.int32, shape, len(shape) - 1)


def pack_kernel(x_ref, keep_ref, far_ref, swap_ref, o_ref):
    me = lax.axis_index("date")
    lane = lanes_of((8, LANES))
    sub = lax.broadcasted_iota(jnp.int32, (8, LANES), 0)
    own = (lane // BLOCK) == (sub % 4)
    places = []
    for q in range(GROUPS):
        p = q ^ me
        places.append(jnp.where(p == 1, 2, jnp.where(p == 2, 1, p)))
    for row in range(ROWS):
        for part in range(2):
            tiles = [
                x_ref[pl.ds(part * 448 + tile * 8 + row, PER, stride=64), :] for tile in range(TILES)
            ]
            zero = jnp.zeros((PER, LANES), jnp.float32)
            for q in range(GROUPS):
                base = (row * 2 + part) * 16
                left = tiles[2 * q - 1] if q > 0 else zero
                right = tiles[2 * q + 2] if q < 3 else zero
                near = jnp.where(lane[:PER] >= LANES - HALF_RG, left, right)
                near = jnp.concatenate([near, jnp.zeros((1, LANES), jnp.float32)], axis=0)
                turned = jnp.zeros((8, LANES), jnp.float32)
                for v in range(4):
                    moved = pltpu.roll(near, HALF_RG + BLOCK * v, 1)
                    turned = jnp.where(own & (sub % 4 == v), moved, turned)
                for half in range(2):
                    o_ref[places[q], pl.ds(base + half * 8, PER), :] = tiles[2 * q + half]
                    line = jnp.sum(turned[4 * half : 4 * half + 4], axis=0, keepdims=True)
                    o_ref[places[q], pl.ds(base + half * 8 + 7, 1), :] = line
    for n in range(0, MIDLEN, 8):
        keep_ref[0, n : n + 8, :] = o_ref[0, n : n + 8, :]
        far_ref[0, n : n + 8, :] = o_ref[1, n : n + 8, :]
        for s in range(2):
            swap_ref[s, n : n + 8, :] = o_ref[2 + s, n : n + 8, :]


class Two(tuple):
    def __add__(self, other):
        return Two((self[0] + other[0], self[1] + other[1]))


def sum_rows(row_of):
    core = row_of(7) + row_of(8) + row_of(9) + row_of(10)
    down = [None] * 8
    down[7] = core
    for r in range(6, -1, -1):
        down[r] = down[r + 1] + row_of(r)
    sums = [down[0]]
    up = None
    for r in range(1, 8):
        row = row_of(r + 10)
        up = row if up is None else up + row
        sums.append(down[r] + up)
    return sums


def split(a, b):
    both = jnp.concatenate([a, b], axis=0)
    high = both.astype(jnp.bfloat16)
    low = (both - high.astype(jnp.float32)).astype(jnp.bfloat16)
    return high, low


def twice(tile, sub):
    turned = pltpu.roll(tile, 7, 0)
    return jnp.where(sub == 7, turned, tile), turned


def fill_band(band):
    for block in range(6):
        src = lax.broadcasted_iota(jnp.int32, (LANES, 256), 0)
        dst = lanes_of((LANES, 256))
        if block < 4:
            hit = jnp.abs(src + (block % 2) * LANES - dst) <= HALF_RG
        else:
            x = src % BLOCK
            col = jnp.where(x < HALF_RG, x - HALF_RG, x - HALF_RG + 256)
            hit = (jnp.abs(col - dst) <= HALF_RG) & (x < 2 * HALF_RG)
        band[block * LANES : (block + 1) * LANES, :] = jnp.where(hit, 1.0, 0.0).astype(jnp.bfloat16)


def slot_of(part, q, half):
    return ((part * 2 + q) * 2 + half) * TALL


def prepare(ref, rows, first, dates, halos):
    lane = lanes_of((8, LANES))
    sub = lax.broadcasted_iota(jnp.int32, (8, LANES), 0)
    for row in range(rows):
        for part in range(2):
            base = (row * 2 + part) * 16
            lines = [[None, None] for _ in range(2)]
            for half in range(2):
                for q in range(2):
                    tile = ref[q, base + half * 8 : base + half * 8 + 8, :]
                    slot = slot_of(part, q, half) + first + row
                    dates[slot, 0:8, :], dates[slot, 8:16, :] = twice(tile, sub)
                    lines[q][half] = jnp.broadcast_to(tile[7:8], (8, LANES))
            lines = [jnp.where(sub < 4, low, high) for low, high in lines]
            by_parity = [
                jnp.where(sub % 2 == 0, lines[0], lines[1]),
                jnp.where(sub % 2 == 0, lines[1], lines[0]),
            ]
            halo = by_parity[0]
            halo = jnp.where(lane // BLOCK == sub % 4, halo, 0.0)
            for e in range(1, 4):
                moved = pltpu.roll(by_parity[e % 2], BLOCK * e, 1)
                halo = jnp.where(lane // BLOCK == (sub + e) % 4, moved, halo)
            for at, tile in zip((0, 8), twice(halo, sub)):
                halos[part * TALL + first + row, at : at + 8, :] = tile


def prepare_all(mid, even, odd, dates, halos):
    upper = lax.axis_index("space") % 2 == 0
    prepare(mid, ROWS, HALF_AZ, dates, halos)
    prepare(even, HALF_AZ, jnp.where(upper, HALF_AZ + ROWS, 0), dates, halos)
    prepare(odd, HALF_AZ, jnp.where(upper, 0, HALF_AZ + ROWS), dates, halos)


def put(lhs, rows, tile, sums):
    for r in range(0, 8, 2):
        high, low = split(sums[r], sums[r + 1])
        lhs[rows + r * 8 : rows + r * 8 + 16, tile * LANES : (tile + 1) * LANES] = high
        lhs[rows + r * 8 : rows + r * 8 + 16, (tile + 2) * LANES : (tile + 3) * LANES] = low


def put_halo(lhs, first, step, sums, count=4):
    blocks = lanes_of((16, LANES)) // BLOCK
    keep = [jnp.where(blocks == q, 1.0, 0.0).astype(jnp.bfloat16) for q in range(count)]
    for r in range(0, 8, 2):
        high, low = split(sums[r], sums[r + 1])
        for q in range(count):
            rows = first + q * step + r * 8
            lhs[rows : rows + 16, 4 * LANES : 5 * LANES] = high * keep[q]
            lhs[rows : rows + 16, 5 * LANES : 6 * LANES] = low * keep[q]


def weigh(dates, halos, band, lhs, weights):
    sub = lax.broadcasted_iota(jnp.int32, (8, LANES), 0)

    def energy(ref, re_slot, im_slot):
        def row_of(row):
            re = ref[re_slot + row, 0:8, :]
            im = ref[im_slot + row, 0:8, :]
            return re * re + im * im

        return sum_rows(row_of)

    for q in range(2):
        for half in range(2):
            put(lhs, q * 64, half, energy(dates, slot_of(0, q, half), slot_of(1, q, half)))
    put_halo(lhs, 0, 64, energy(halos, 0, TALL), 2)
    power = jnp.dot(lhs[0:128, :], band[...], preferred_element_type=jnp.float32)
    root = lax.rsqrt(power)
    for q in range(2):
        for r in range(8):
            for half in range(2):
                tile = root[q * 64 + r * 8 : q * 64 + r * 8 + 8, half * LANES : (half + 1) * LANES]
                slot = (q * 8 + r) * 2 + half
                weights[slot, 0:8, :], weights[slot, 8:16, :] = twice(tile, sub)


def cross_rows(load_i, load_j):
    def row_of(row):
        (are, aim), (bre, bim) = load_i(row), load_j(row)
        return Two((are * bre + aim * bim, aim * bre - are * bim))

    return sum_rows(row_of)


def main_tile(ref, q, half, m):
    re, im = slot_of(0, q, half), slot_of(1, q, half)
    return lambda row: (ref[re + row, pl.ds(m, 8), :], ref[im + row, pl.ds(m, 8), :])


def build_main(lhs, at, left, right, m):
    for half in range(2):
        sums = cross_rows(main_tile(*left, half, 0), main_tile(*right, half, m))
        put(lhs, at, half, [s[0] for s in sums])
        put(lhs, at + 64, half, [s[1] for s in sums])


def build_halo(lhs, load_i, load_j):
    sums = cross_rows(load_i, load_j)
    put_halo(lhs, 0, 128, [s[0] for s in sums])
    put_halo(lhs, 64, 128, [s[1] for s in sums])


def finish(lhs, band, weigh_of, res, base):
    boxed = jnp.dot(lhs[...], band[...], preferred_element_type=jnp.float32)
    for q in range(4):
        (wi_ref, wi_q), (wj_ref, wj_q), m = weigh_of(q)
        for r in range(8):
            for half in range(2):
                cols = slice(half * LANES, (half + 1) * LANES)
                re = boxed[q * 128 + r * 8 : q * 128 + r * 8 + 8, cols]
                im = boxed[q * 128 + 64 + r * 8 : q * 128 + 64 + r * 8 + 8, cols]
                square = re * re + im * im
                size = square * lax.rsqrt(jnp.maximum(square, TINY))
                wi = wi_ref[(wi_q * 8 + r) * 2 + half, 0:8, :]
                wj = wj_ref[(wj_q * 8 + r) * 2 + half, pl.ds(m, 8), :]
                start = pl.multiple_of(base + q * 128 + half * 64 + r * 8, 8)
                res[pl.ds(start, 8), :] = size * wi * wj


def inner_unit(n, dates, halos):
    lane = lanes_of((8, LANES))
    pair = INNER[2 * n : 2 * n + 2]

    def build(lhs):
        for s, (same, m) in enumerate(pair):
            for q in range(2):
                other = q if same else 1 - q
                build_main(lhs, (s * 2 + q) * 128, (dates, q), (dates, other), m)

        def load_i(row):
            return halos[row, 0:8, :], halos[TALL + row, 0:8, :]

        def load_j(row):
            out = []
            for part in range(2):
                tiles = []
                for same, m in pair:
                    tile = halos[part * TALL + row, pl.ds(m, 8), :]
                    tiles.append(tile if same else pltpu.roll(tile, BLOCK, 1))
                out.append(jnp.where(lane < 2 * BLOCK, tiles[0], tiles[1]))
            return out

        build_halo(lhs, load_i, load_j)

    def weigh_of(weights):
        def of(q):
            same, m = pair[q // 2]
            return (weights, q % 2), (weights, q % 2 if same else 1 - q % 2), m

        return of

    return build, weigh_of


def near_kernel(mid, even, odd, dates, halos, weights, band, res, lhs_a, lhs_b):
    fill_band(band)
    prepare_all(mid, even, odd, dates, halos)
    weigh(dates, halos, band, lhs_b, weights)
    units = [inner_unit(n, dates, halos) for n in range(4)]
    buffers = [lhs_a, lhs_b]
    units[0][0](buffers[0])
    for n in range(4):
        if n < 3:
            units[n + 1][0](buffers[(n + 1) % 2])
        finish(buffers[n % 2], band, units[n][1](weights), res, n * 512)


def far_kernel(
    table, mid, even, odd, dates_n, halos_n, weights_n, band, res_n, o_ref,
    dates_f, halos_f, halos_o, weights_f, lhs_a, lhs_b, res, out, sems,
):
    lane = lanes_of((8, LANES))
    prepare_all(mid, even, odd, dates_f, halos_f)
    weigh(dates_f, halos_f, band, lhs_b, weights_f)
    for n in range(0, NEAR_ROWS, 8):
        res[n : n + 8, :] = res_n[n : n + 8, :]

    units = [inner_unit(n, dates_f, halos_f) for n in range(4)]
    sides_d = [(dates_n, 0), (dates_n, 1), (dates_f, 0), (dates_f, 1)]
    sides_w = [(weights_n, 0), (weights_n, 1), (weights_f, 0), (weights_f, 1)]

    for part in range(2):
        for row in range(TALL):
            slot = part * TALL + row
            for at in (0, 8):
                near = halos_n[slot, at : at + 8, :]
                far = halos_f[slot, at : at + 8, :]
                if at == 0:
                    halos_o[slot, 0:8, :] = jnp.where(lane < 2 * BLOCK, near, far)
                near = pltpu.roll(near, BLOCK, 1)
                halos_o[2 * TALL + slot, at : at + 8, :] = jnp.where(lane < 2 * BLOCK, far, near)

    def outer_build(m, lhs):
        for q, (pi, pj) in enumerate(OUTER):
            build_main(lhs, q * 128, sides_d[pi], sides_d[pj], m)
        build_halo(
            lhs,
            lambda row: (halos_o[row, 0:8, :], halos_o[TALL + row, 0:8, :]),
            lambda row: (
                halos_o[2 * TALL + row, pl.ds(m, 8), :],
                halos_o[3 * TALL + row, pl.ds(m, 8), :],
            ),
        )

    def outer_finish(m, lhs):
        def of(q):
            pi, pj = OUTER[q]
            return sides_w[pi], sides_w[pj], m

        finish(lhs, band, of, res, 2 * NEAR_ROWS + m * 512)

    buffers = [lhs_a, lhs_b]
    units[0][0](buffers[0])
    for n in range(4):
        if n < 3:
            units[n + 1][0](buffers[(n + 1) % 2])
        else:
            outer_build(0, lhs_a)
        finish(buffers[n % 2], band, units[n][1](weights_f), res, NEAR_ROWS + n * 512)

    def two(s, carry):
        outer_build(2 * s + 1, lhs_b)
        outer_finish(2 * s, lhs_a)
        outer_build(2 * s + 2, lhs_a)
        outer_finish(2 * s + 1, lhs_b)
        return carry

    lax.fori_loop(0, 3, two, 0)
    outer_finish(6, lhs_a)

    mine = lax.axis_index("date") * (LAGS * DATES)
    size = DATES * 16

    def copy_of(k):
        rows = pl.ds(pl.multiple_of(k * size, size), size)
        return pltpu.make_async_copy(out.at[rows], o_ref.at[rows], sems.at[k])

    def emit(k, carry):
        for i in range(DATES):
            start = table[mine + k * DATES + i]
            for half in range(2):
                target = pl.multiple_of(k * size + i * 16 + half * 8, 8)
                out[pl.ds(target, 8), :] = res[pl.ds(start + half * 64, 8, stride=8), :]
        copy_of(k).start()
        return carry

    lax.fori_loop(0, LAGS, emit, 0)

    def settle(k, carry):
        copy_of(k).wait()
        return carry

    lax.fori_loop(0, LAGS, settle, 0)


VMEM = pl.BlockSpec(memory_space=pltpu.VMEM)
DATES_SHAPE = (2 * 2 * 2 * TALL, 16, LANES)
HALOS_SHAPE = (2 * TALL, 16, LANES)
WEIGHTS_SHAPE = (2 * 8 * 2, 16, LANES)
BAND_SHAPE = (6 * LANES, 256)
LHS_SHAPE = (512, 6 * LANES)


def pack(stack):
    flat = stack.reshape(2, PER, ROWS, TILES, LANES).transpose(0, 1, 3, 2, 4).reshape(-1, LANES)
    return pl.pallas_call(
        pack_kernel,
        out_shape=[jax.ShapeDtypeStruct((n, MIDLEN, LANES), jnp.float32) for n in (1, 1, 2)],
        in_specs=[VMEM],
        out_specs=[VMEM] * 3,
        scratch_shapes=[pltpu.VMEM((GROUPS, MIDLEN, LANES), jnp.float32)],
        compiler_params=pltpu.CompilerParams(vmem_limit_bytes=4 * 1024 * 1024),
        name="pack",
    )(flat)


def near_part(mid, even, odd):
    shapes = [
        (DATES_SHAPE, jnp.float32),
        (HALOS_SHAPE, jnp.float32),
        (WEIGHTS_SHAPE, jnp.float32),
        (BAND_SHAPE, jnp.bfloat16),
        ((NEAR_ROWS, LANES), jnp.float32),
    ]
    return pl.pallas_call(
        near_kernel,
        out_shape=[jax.ShapeDtypeStruct(shape, dtype) for shape, dtype in shapes],
        in_specs=[VMEM] * 3,
        out_specs=[VMEM] * 5,
        scratch_shapes=[pltpu.VMEM(LHS_SHAPE, jnp.bfloat16)] * 2,
        compiler_params=pltpu.CompilerParams(vmem_limit_bytes=16 * 1024 * 1024),
        cost_estimate=pl.CostEstimate(flops=1_600_000_000, bytes_accessed=6_000_000, transcendentals=0),
        name="near",
    )(mid, even, odd)


def far_part(mid, even, odd, near):
    out = pl.pallas_call(
        far_kernel,
        out_shape=jax.ShapeDtypeStruct((LAGS * DATES * 2 * 8, LANES), jnp.float32),
        in_specs=[pl.BlockSpec(memory_space=pltpu.SMEM)] + [VMEM] * 8,
        out_specs=pl.BlockSpec(memory_space=pl.ANY),
        scratch_shapes=[
            pltpu.VMEM(DATES_SHAPE, jnp.float32),
            pltpu.VMEM(HALOS_SHAPE, jnp.float32),
            pltpu.VMEM((4 * TALL, 16, LANES), jnp.float32),
            pltpu.VMEM(WEIGHTS_SHAPE, jnp.float32),
            pltpu.VMEM(LHS_SHAPE, jnp.bfloat16),
            pltpu.VMEM(LHS_SHAPE, jnp.bfloat16),
            pltpu.VMEM((RES_ROWS, LANES), jnp.float32),
            pltpu.VMEM((LAGS * DATES * 2 * 8, LANES), jnp.float32),
            pltpu.SemaphoreType.DMA((LAGS,)),
        ],
        compiler_params=pltpu.CompilerParams(vmem_limit_bytes=32 * 1024 * 1024),
        cost_estimate=pl.CostEstimate(flops=4_800_000_000, bytes_accessed=9_000_000, transcendentals=0),
        name="far",
    )(jnp.asarray(lag_tables()), mid, even, odd, *near)
    return (
        out.reshape(LAGS, DATES, 2, ROWS, LANES)
        .transpose(0, 1, 3, 2, 4)
        .reshape(LAGS, DATES, ROWS, 2 * LANES)
    )


def body(stack):
    peers = lax.axis_size("space")
    sibling = [(i, i ^ 1) for i in range(GROUPS)]
    across = [(i, i ^ 2) for i in range(GROUPS)]
    even_pairs = [(i, i ^ 1) for i in range(peers)]
    odd_pairs = [(i, i + 1) for i in range(1, peers - 1, 2)]
    odd_pairs += [(j, i) for i, j in odd_pairs]
    upper = lax.axis_index("space") % 2 == 0

    def row_halos(mid):
        first, last = mid[:, :HALOLEN], mid[:, MIDLEN - HALOLEN :]
        odd = lax.ppermute(jnp.where(upper, first, last), "space", odd_pairs)
        even = lax.ppermute(jnp.where(upper, last, first), "space", even_pairs)
        return even, odd

    kept, sent, swap = pack(stack)
    swapped = lax.ppermute(swap, "date", sibling)
    far = lax.ppermute(jnp.concatenate([sent, swapped[1:2]]), "date", across)
    near = jnp.concatenate([kept, swapped[0:1]])
    done = near_part(near, *row_halos(near))
    return far_part(far, *row_halos(far), done)


def solution(mesh):
    in_specs = (P(None, "date", "space", None),)
    out_specs = P(None, None, "space", "date")
    return jax.shard_map(body, mesh=mesh, in_specs=in_specs, out_specs=out_specs, check_vma=False)
```

```python
import jax
import jax.numpy as jnp
import numpy as np
from jax import lax
from jax.experimental import pallas as pl
from jax.experimental.pallas import tpu as pltpu
from jax.sharding import PartitionSpec as P

WIN_AZ = 11
WIN_RG = 23
HALF_AZ = WIN_AZ // 2
HALF_RG = WIN_RG // 2
DATES = 28
LAGS = 14
GROUPS = 4
PER = 7
ROWS = 8
PLANE = 16
TALL = ROWS + 2 * HALF_AZ
BLOCK = 32
TILES = GROUPS * 2
LANES = 128
ROWLEN = 2 * 2 * 8
MIDLEN = ROWS * ROWLEN
HALOLEN = HALF_AZ * ROWLEN
TINY = float(np.finfo(np.float32).tiny)

INNER = [(True, m) for m in (1, 2, 3)] + [(False, m) for m in range(4)]
OUTER = [(0, 2), (1, 3), (2, 1), (3, 0)]
NEAR_ROWS = len(INNER) * 2 * 128
RES_ROWS = 2 * NEAR_ROWS + 7 * 4 * 128


def lag_tables():
    out = []
    for a in range(GROUPS):
        where = {}

        def note(start, pi, pj, m):
            for u in range(PER):
                i, j = 7 * (pi ^ a) + u, 7 * (pj ^ a) + (u + m) % 7
                where.setdefault((i, j), start + u)
                where.setdefault((j, i), start + u)

        for far in range(2):
            for n, (same, m) in enumerate(INNER):
                for q in range(2):
                    p = 2 * far + q
                    note(far * NEAR_ROWS + (n * 2 + q) * 128, p, p if same else p ^ 1, m)
        for m in range(7):
            for q, (pi, pj) in enumerate(OUTER):
                note(2 * NEAR_ROWS + (m * 4 + q) * 128, pi, pj, m)
        out += [where[(i, (i + k + 1) % DATES)] for k in range(LAGS) for i in range(DATES)]
    return np.array(out, np.int32)


def lanes_of(shape):
    return lax.broadcasted_iota(jnp.int32, shape, len(shape) - 1)


def pack_kernel(x_ref, keep_ref, far_ref, swap_ref, o_ref):
    me = lax.axis_index("date")
    lane = lanes_of((8, LANES))
    sub = lax.broadcasted_iota(jnp.int32, (8, LANES), 0)
    own = (lane // BLOCK) == (sub % 4)
    places = []
    for q in range(GROUPS):
        p = q ^ me
        places.append(jnp.where(p == 1, 2, jnp.where(p == 2, 1, p)))
    for row in range(ROWS):
        for part in range(2):
            tiles = [
                x_ref[pl.ds(part * 448 + tile * 8 + row, PER, stride=64), :] for tile in range(TILES)
            ]
            zero = jnp.zeros((PER, LANES), jnp.float32)
            for q in range(GROUPS):
                base = (row * 2 + part) * 16
                left = tiles[2 * q - 1] if q > 0 else zero
                right = tiles[2 * q + 2] if q < 3 else zero
                near = jnp.where(lane[:PER] >= LANES - HALF_RG, left, right)
                near = jnp.concatenate([near, jnp.zeros((1, LANES), jnp.float32)], axis=0)
                turned = jnp.zeros((8, LANES), jnp.float32)
                for v in range(4):
                    moved = pltpu.roll(near, HALF_RG + BLOCK * v, 1)
                    turned = jnp.where(own & (sub % 4 == v), moved, turned)
                for half in range(2):
                    o_ref[places[q], pl.ds(base + half * 8, PER), :] = tiles[2 * q + half]
                    line = jnp.sum(turned[4 * half : 4 * half + 4], axis=0, keepdims=True)
                    o_ref[places[q], pl.ds(base + half * 8 + 7, 1), :] = line
    for n in range(0, MIDLEN, 8):
        keep_ref[0, n : n + 8, :] = o_ref[0, n : n + 8, :]
        far_ref[0, n : n + 8, :] = o_ref[1, n : n + 8, :]
        for s in range(2):
            swap_ref[s, n : n + 8, :] = o_ref[2 + s, n : n + 8, :]


class Two(tuple):
    def __add__(self, other):
        return Two((self[0] + other[0], self[1] + other[1]))


def sum_rows(row_of):
    core = row_of(7) + row_of(8) + row_of(9) + row_of(10)
    down = [None] * 8
    down[7] = core
    for r in range(6, -1, -1):
        down[r] = down[r + 1] + row_of(r)
    sums = [down[0]]
    up = None
    for r in range(1, 8):
        row = row_of(r + 10)
        up = row if up is None else up + row
        sums.append(down[r] + up)
    return sums


def split(a, b):
    both = jnp.concatenate([a, b], axis=0)
    high = both.astype(jnp.bfloat16)
    low = (both - high.astype(jnp.float32)).astype(jnp.bfloat16)
    return high, low


def twice(tile, sub):
    turned = pltpu.roll(tile, 7, 0)
    return jnp.where(sub == 7, turned, tile), turned


def fill_band(band):
    for block in range(6):
        src = lax.broadcasted_iota(jnp.int32, (LANES, 256), 0)
        dst = lanes_of((LANES, 256))
        if block < 4:
            hit = jnp.abs(src + (block % 2) * LANES - dst) <= HALF_RG
        else:
            x = src % BLOCK
            col = jnp.where(x < HALF_RG, x - HALF_RG, x - HALF_RG + 256)
            hit = (jnp.abs(col - dst) <= HALF_RG) & (x < 2 * HALF_RG)
        band[block * LANES : (block + 1) * LANES, :] = jnp.where(hit, 1.0, 0.0).astype(jnp.bfloat16)


def slot_of(part, q, half):
    return ((part * 2 + q) * 2 + half) * TALL


def prepare(refs, rows, first, dates, halos):
    lane = lanes_of((8, LANES))
    sub = lax.broadcasted_iota(jnp.int32, (8, LANES), 0)
    for row in range(rows):
        for part in range(2):
            base = (row * 2 + part) * 16
            lines = [[None, None] for _ in range(2)]
            for half in range(2):
                for q in range(2):
                    tile = refs[0][q, base + half * 8 : base + half * 8 + 8, :]
                    for ref in refs[1:]:
                        tile = tile + ref[q, base + half * 8 : base + half * 8 + 8, :]
                    slot = slot_of(part, q, half) + first + row
                    dates[slot, 0:8, :], dates[slot, 8:16, :] = twice(tile, sub)
                    lines[q][half] = jnp.broadcast_to(tile[7:8], (8, LANES))
            lines = [jnp.where(sub < 4, low, high) for low, high in lines]
            by_parity = [
                jnp.where(sub % 2 == 0, lines[0], lines[1]),
                jnp.where(sub % 2 == 0, lines[1], lines[0]),
            ]
            halo = by_parity[0]
            halo = jnp.where(lane // BLOCK == sub % 4, halo, 0.0)
            for e in range(1, 4):
                moved = pltpu.roll(by_parity[e % 2], BLOCK * e, 1)
                halo = jnp.where(lane // BLOCK == (sub + e) % 4, moved, halo)
            for at, tile in zip((0, 8), twice(halo, sub)):
                halos[part * TALL + first + row, at : at + 8, :] = tile


def prepare_all(mid, even, odd, dates, halos):
    upper = lax.axis_index("space") % 2 == 0
    prepare([mid], ROWS, HALF_AZ, dates, halos)
    prepare([even], HALF_AZ, jnp.where(upper, HALF_AZ + ROWS, 0), dates, halos)
    prepare(odd, HALF_AZ, jnp.where(upper, 0, HALF_AZ + ROWS), dates, halos)


def put(lhs, rows, tile, sums):
    for r in range(0, 8, 2):
        high, low = split(sums[r], sums[r + 1])
        lhs[rows + r * 8 : rows + r * 8 + 16, tile * LANES : (tile + 1) * LANES] = high
        lhs[rows + r * 8 : rows + r * 8 + 16, (tile + 2) * LANES : (tile + 3) * LANES] = low


def put_halo(lhs, first, step, sums, count=4):
    blocks = lanes_of((16, LANES)) // BLOCK
    keep = [jnp.where(blocks == q, 1.0, 0.0).astype(jnp.bfloat16) for q in range(count)]
    for r in range(0, 8, 2):
        high, low = split(sums[r], sums[r + 1])
        for q in range(count):
            rows = first + q * step + r * 8
            lhs[rows : rows + 16, 4 * LANES : 5 * LANES] = high * keep[q]
            lhs[rows : rows + 16, 5 * LANES : 6 * LANES] = low * keep[q]


def weigh(dates, halos, band, lhs, weights):
    sub = lax.broadcasted_iota(jnp.int32, (8, LANES), 0)

    def energy(ref, re_slot, im_slot):
        def row_of(row):
            re = ref[re_slot + row, 0:8, :]
            im = ref[im_slot + row, 0:8, :]
            return re * re + im * im

        return sum_rows(row_of)

    for q in range(2):
        for half in range(2):
            put(lhs, q * 64, half, energy(dates, slot_of(0, q, half), slot_of(1, q, half)))
    put_halo(lhs, 0, 64, energy(halos, 0, TALL), 2)
    power = jnp.dot(lhs[0:128, :], band[...], preferred_element_type=jnp.float32)
    root = lax.rsqrt(power)
    for q in range(2):
        for r in range(8):
            for half in range(2):
                tile = root[q * 64 + r * 8 : q * 64 + r * 8 + 8, half * LANES : (half + 1) * LANES]
                slot = (q * 8 + r) * 2 + half
                weights[slot, 0:8, :], weights[slot, 8:16, :] = twice(tile, sub)


def cross_rows(load_i, load_j):
    def row_of(row):
        (are, aim), (bre, bim) = load_i(row), load_j(row)
        return Two((are * bre + aim * bim, aim * bre - are * bim))

    return sum_rows(row_of)


def main_tile(ref, q, half, m):
    re, im = slot_of(0, q, half), slot_of(1, q, half)
    return lambda row: (ref[re + row, pl.ds(m, 8), :], ref[im + row, pl.ds(m, 8), :])


def build_main(lhs, at, left, right, m):
    for half in range(2):
        sums = cross_rows(main_tile(*left, half, 0), main_tile(*right, half, m))
        put(lhs, at, half, [s[0] for s in sums])
        put(lhs, at + 64, half, [s[1] for s in sums])


def build_halo(lhs, load_i, load_j, count=4):
    sums = cross_rows(load_i, load_j)
    put_halo(lhs, 0, 128, [s[0] for s in sums], count)
    put_halo(lhs, 64, 128, [s[1] for s in sums], count)


def finish(lhs, band, weigh_of, res, base, count=4):
    boxed = jnp.dot(lhs[0 : count * 128, :], band[...], preferred_element_type=jnp.float32)
    for q in range(count):
        (wi_ref, wi_q), (wj_ref, wj_q), m = weigh_of(q)
        for r in range(8):
            for half in range(2):
                cols = slice(half * LANES, (half + 1) * LANES)
                re = boxed[q * 128 + r * 8 : q * 128 + r * 8 + 8, cols]
                im = boxed[q * 128 + 64 + r * 8 : q * 128 + 64 + r * 8 + 8, cols]
                square = re * re + im * im
                size = square * lax.rsqrt(jnp.maximum(square, TINY))
                wi = wi_ref[(wi_q * 8 + r) * 2 + half, 0:8, :]
                wj = wj_ref[(wj_q * 8 + r) * 2 + half, pl.ds(m, 8), :]
                start = pl.multiple_of(base + q * 128 + half * 64 + r * 8, 8)
                res[pl.ds(start, 8), :] = size * wi * wj


def inner_unit(n, dates, halos):
    lane = lanes_of((8, LANES))
    pair = INNER[2 * n : 2 * n + 2]

    def build(lhs):
        for s, (same, m) in enumerate(pair):
            for q in range(2):
                other = q if same else 1 - q
                build_main(lhs, (s * 2 + q) * 128, (dates, q), (dates, other), m)

        def load_i(row):
            return halos[row, 0:8, :], halos[TALL + row, 0:8, :]

        def load_j(row):
            out = []
            for part in range(2):
                tiles = []
                for same, m in pair:
                    tile = halos[part * TALL + row, pl.ds(m, 8), :]
                    tiles.append(tile if same else pltpu.roll(tile, BLOCK, 1))
                out.append(jnp.where(lane < 2 * BLOCK, tiles[0], tiles[-1]) if len(tiles) > 1 else tiles[0])
            return out

        build_halo(lhs, load_i, load_j, 2 * len(pair))

    def weigh_of(weights):
        def of(q):
            same, m = pair[q // 2]
            return (weights, q % 2), (weights, q % 2 if same else 1 - q % 2), m

        return of

    return build, weigh_of


def near_kernel(mid, even, odd, dates, halos, weights, band, res, lhs_a, lhs_b):
    fill_band(band)
    prepare_all(mid, even, [odd], dates, halos)
    weigh(dates, halos, band, lhs_b, weights)
    units = [inner_unit(n, dates, halos) for n in range(4)]
    buffers = [lhs_a, lhs_b]
    units[0][0](buffers[0])
    for n in range(4):
        if n < 3:
            units[n + 1][0](buffers[(n + 1) % 2])
        finish(buffers[n % 2], band, units[n][1](weights), res, n * 512, min(4, 2 * (len(INNER) - 2 * n)))


def far_kernel(
    table, mid, even, odd, odd_far, dates_n, halos_n, weights_n, band, res_n, o_ref,
    dates_f, halos_f, halos_o, weights_f, lhs_a, lhs_b, res, out, sems,
):
    lane = lanes_of((8, LANES))
    prepare_all(mid, even, [odd, odd_far], dates_f, halos_f)
    weigh(dates_f, halos_f, band, lhs_b, weights_f)
    for n in range(0, NEAR_ROWS, 8):
        res[n : n + 8, :] = res_n[n : n + 8, :]

    units = [inner_unit(n, dates_f, halos_f) for n in range(4)]
    sides_d = [(dates_n, 0), (dates_n, 1), (dates_f, 0), (dates_f, 1)]
    sides_w = [(weights_n, 0), (weights_n, 1), (weights_f, 0), (weights_f, 1)]

    for part in range(2):
        for row in range(TALL):
            slot = part * TALL + row
            for at in (0, 8):
                near = halos_n[slot, at : at + 8, :]
                far = halos_f[slot, at : at + 8, :]
                if at == 0:
                    halos_o[slot, 0:8, :] = jnp.where(lane < 2 * BLOCK, near, far)
                near = pltpu.roll(near, BLOCK, 1)
                halos_o[2 * TALL + slot, at : at + 8, :] = jnp.where(lane < 2 * BLOCK, far, near)

    def outer_build(m, lhs):
        for q, (pi, pj) in enumerate(OUTER):
            build_main(lhs, q * 128, sides_d[pi], sides_d[pj], m)
        build_halo(
            lhs,
            lambda row: (halos_o[row, 0:8, :], halos_o[TALL + row, 0:8, :]),
            lambda row: (
                halos_o[2 * TALL + row, pl.ds(m, 8), :],
                halos_o[3 * TALL + row, pl.ds(m, 8), :],
            ),
        )

    def outer_finish(m, lhs):
        def of(q):
            pi, pj = OUTER[q]
            return sides_w[pi], sides_w[pj], m

        finish(lhs, band, of, res, 2 * NEAR_ROWS + m * 512)

    buffers = [lhs_a, lhs_b]
    units[0][0](buffers[0])
    for n in range(4):
        if n < 3:
            units[n + 1][0](buffers[(n + 1) % 2])
        else:
            outer_build(0, lhs_a)
        finish(buffers[n % 2], band, units[n][1](weights_f), res, NEAR_ROWS + n * 512, min(4, 2 * (len(INNER) - 2 * n)))

    for m in range(7):
        if m < 6:
            outer_build(m + 1, buffers[(m + 1) % 2])
        outer_finish(m, buffers[m % 2])

    mine = lax.axis_index("date") * (LAGS * DATES)
    size = DATES * 16

    def copy_of(k):
        rows = pl.ds(pl.multiple_of(k * size, size), size)
        return pltpu.make_async_copy(out.at[rows], o_ref.at[rows], sems.at[k])

    def emit(k, carry):
        for i in range(DATES):
            start = table[mine + k * DATES + i]
            for half in range(2):
                target = pl.multiple_of(k * size + i * 16 + half * 8, 8)
                out[pl.ds(target, 8), :] = res[pl.ds(start + half * 64, 8, stride=8), :]
        copy_of(k).start()
        return carry

    lax.fori_loop(0, LAGS, emit, 0)

    def settle(k, carry):
        copy_of(k).wait()
        return carry

    lax.fori_loop(0, LAGS, settle, 0)


VMEM = pl.BlockSpec(memory_space=pltpu.VMEM)
DATES_SHAPE = (2 * 2 * 2 * TALL, 16, LANES)
HALOS_SHAPE = (2 * TALL, 16, LANES)
WEIGHTS_SHAPE = (2 * 8 * 2, 16, LANES)
BAND_SHAPE = (6 * LANES, 256)
LHS_SHAPE = (512, 6 * LANES)


def pack(stack):
    flat = stack.reshape(2, PER, ROWS, TILES, LANES).transpose(0, 1, 3, 2, 4).reshape(-1, LANES)
    return pl.pallas_call(
        pack_kernel,
        out_shape=[jax.ShapeDtypeStruct((n, MIDLEN, LANES), jnp.float32) for n in (1, 1, 2)],
        in_specs=[VMEM],
        out_specs=[VMEM] * 3,
        scratch_shapes=[pltpu.VMEM((GROUPS, MIDLEN, LANES), jnp.float32)],
        compiler_params=pltpu.CompilerParams(vmem_limit_bytes=4 * 1024 * 1024),
        name="pack",
    )(flat)


def near_part(mid, even, odd):
    shapes = [
        (DATES_SHAPE, jnp.float32),
        (HALOS_SHAPE, jnp.float32),
        (WEIGHTS_SHAPE, jnp.float32),
        (BAND_SHAPE, jnp.bfloat16),
        ((NEAR_ROWS, LANES), jnp.float32),
    ]
    return pl.pallas_call(
        near_kernel,
        out_shape=[jax.ShapeDtypeStruct(shape, dtype) for shape, dtype in shapes],
        in_specs=[VMEM] * 3,
        out_specs=[VMEM] * 5,
        scratch_shapes=[pltpu.VMEM(LHS_SHAPE, jnp.bfloat16)] * 2,
        compiler_params=pltpu.CompilerParams(vmem_limit_bytes=16 * 1024 * 1024),
        cost_estimate=pl.CostEstimate(flops=1_600_000_000, bytes_accessed=6_000_000, transcendentals=0),
        name="near",
    )(mid, even, odd)


def far_part(mid, even, odd, odd_far, near):
    out = pl.pallas_call(
        far_kernel,
        out_shape=jax.ShapeDtypeStruct((LAGS * DATES * 2 * 8, LANES), jnp.float32),
        in_specs=[pl.BlockSpec(memory_space=pltpu.SMEM)] + [VMEM] * 9,
        out_specs=pl.BlockSpec(memory_space=pl.ANY),
        scratch_shapes=[
            pltpu.VMEM(DATES_SHAPE, jnp.float32),
            pltpu.VMEM(HALOS_SHAPE, jnp.float32),
            pltpu.VMEM((4 * TALL, 16, LANES), jnp.float32),
            pltpu.VMEM(WEIGHTS_SHAPE, jnp.float32),
            pltpu.VMEM(LHS_SHAPE, jnp.bfloat16),
            pltpu.VMEM(LHS_SHAPE, jnp.bfloat16),
            pltpu.VMEM((RES_ROWS, LANES), jnp.float32),
            pltpu.VMEM((LAGS * DATES * 2 * 8, LANES), jnp.float32),
            pltpu.SemaphoreType.DMA((LAGS,)),
        ],
        compiler_params=pltpu.CompilerParams(vmem_limit_bytes=32 * 1024 * 1024),
        cost_estimate=pl.CostEstimate(flops=4_800_000_000, bytes_accessed=9_000_000, transcendentals=0),
        name="far",
    )(jnp.asarray(lag_tables()), mid, even, odd, odd_far, *near)
    return (
        out.reshape(LAGS, DATES, 2, ROWS, LANES)
        .transpose(0, 1, 3, 2, 4)
        .reshape(LAGS, DATES, ROWS, 2 * LANES)
    )


def body(stack):
    peers = lax.axis_size("space")
    sibling = [(i, i ^ 1) for i in range(GROUPS)]
    across = [(i, i ^ 2) for i in range(GROUPS)]
    even_pairs = [(i, i ^ 1) for i in range(peers)]
    odd_pairs = [(i, i + 1) for i in range(1, peers - 1, 2)]
    odd_pairs += [(j, i) for i, j in odd_pairs]
    flat_pairs = [(i, j) for i, j in odd_pairs if i // PLANE == j // PLANE]
    cross_pairs = [
        (d * peers + i, (d ^ 2) * peers + j)
        for d in range(GROUPS)
        for i, j in odd_pairs
        if i // PLANE != j // PLANE
    ]
    upper = lax.axis_index("space") % 2 == 0

    def edges(mid):
        first, last = mid[:, :HALOLEN], mid[:, MIDLEN - HALOLEN :]
        return jnp.where(upper, first, last), jnp.where(upper, last, first)

    kept, sent, swap = pack(stack)
    swapped = lax.ppermute(swap, "date", sibling)
    away = jnp.concatenate([sent, swapped[1:2]])
    far = lax.ppermute(away, "date", across)
    near = jnp.concatenate([kept, swapped[0:1]])
    near_odd, near_even = edges(near)
    near_odd = lax.ppermute(near_odd, "space", odd_pairs)
    far_cross = lax.ppermute(edges(away)[0], ("date", "space"), cross_pairs)
    near_even = lax.ppermute(near_even, "space", even_pairs)
    far_odd, far_even = edges(far)
    far_odd = lax.ppermute(far_odd, "space", flat_pairs)
    far_even = lax.ppermute(far_even, "space", even_pairs)
    return far_part(far, far_even, far_odd, far_cross, near_part(near, near_even, near_odd))


def solution(mesh):
    in_specs = (P(None, "date", "space", None),)
    out_specs = P(None, None, "space", "date")
    return jax.shard_map(body, mesh=mesh, in_specs=in_specs, out_specs=out_specs, check_vma=False)
```

```python
import jax
import jax.numpy as jnp
import numpy as np
from jax import lax
from jax.experimental import pallas as pl
from jax.experimental.pallas import tpu as pltpu
from jax.sharding import PartitionSpec as P

WIN_AZ = 11
WIN_RG = 23
HALF_AZ = WIN_AZ // 2
HALF_RG = WIN_RG // 2
DATES = 28
LAGS = 14
GROUPS = 4
PER = 7
ROWS = 8
PLANE = 16
TALL = ROWS + 2 * HALF_AZ
BLOCK = 32
TILES = GROUPS * 2
LANES = 128
ROWLEN = 2 * 2 * 8
MIDLEN = ROWS * ROWLEN
HALOLEN = HALF_AZ * ROWLEN
TINY = float(np.finfo(np.float32).tiny)

INNER = [(True, m) for m in (1, 2, 3)] + [(False, m) for m in range(4)]
OUTER = [(0, 2), (1, 3), (2, 1), (3, 0)]
NEAR_ROWS = len(INNER) * 2 * 128
RES_ROWS = 2 * NEAR_ROWS + 7 * 4 * 128


def lag_tables():
    out = []
    for a in range(GROUPS):
        where = {}

        def note(start, pi, pj, m):
            for u in range(PER):
                i, j = 7 * (pi ^ a) + u, 7 * (pj ^ a) + (u + m) % 7
                where.setdefault((i, j), start + u)
                where.setdefault((j, i), start + u)

        for far in range(2):
            for n, (same, m) in enumerate(INNER):
                for q in range(2):
                    p = 2 * far + q
                    note(far * NEAR_ROWS + (n * 2 + q) * 128, p, p if same else p ^ 1, m)
        for m in range(7):
            for q, (pi, pj) in enumerate(OUTER):
                note(2 * NEAR_ROWS + (m * 4 + q) * 128, pi, pj, m)
        out += [where[(i, (i + k + 1) % DATES)] for k in range(LAGS) for i in range(DATES)]
    return np.array(out, np.int32)


def lanes_of(shape):
    return lax.broadcasted_iota(jnp.int32, shape, len(shape) - 1)


def pack_kernel(x_ref, keep_ref, far_ref, swap_ref, o_ref):
    me = lax.axis_index("date")
    lane = lanes_of((8, LANES))
    sub = lax.broadcasted_iota(jnp.int32, (8, LANES), 0)
    own = (lane // BLOCK) == (sub % 4)
    places = []
    for q in range(GROUPS):
        p = q ^ me
        places.append(jnp.where(p == 1, 2, jnp.where(p == 2, 1, p)))
    for row in range(ROWS):
        for part in range(2):
            tiles = [
                x_ref[pl.ds(part * 448 + tile * 8 + row, PER, stride=64), :] for tile in range(TILES)
            ]
            zero = jnp.zeros((PER, LANES), jnp.float32)
            for q in range(GROUPS):
                base = (row * 2 + part) * 16
                left = tiles[2 * q - 1] if q > 0 else zero
                right = tiles[2 * q + 2] if q < 3 else zero
                near = jnp.where(lane[:PER] >= LANES - HALF_RG, left, right)
                near = jnp.concatenate([near, jnp.zeros((1, LANES), jnp.float32)], axis=0)
                turned = jnp.zeros((8, LANES), jnp.float32)
                for v in range(4):
                    moved = pltpu.roll(near, HALF_RG + BLOCK * v, 1)
                    turned = jnp.where(own & (sub % 4 == v), moved, turned)
                for half in range(2):
                    o_ref[places[q], pl.ds(base + half * 8, PER), :] = tiles[2 * q + half]
                    line = jnp.sum(turned[4 * half : 4 * half + 4], axis=0, keepdims=True)
                    o_ref[places[q], pl.ds(base + half * 8 + 7, 1), :] = line
    for n in range(0, MIDLEN, 8):
        keep_ref[0, n : n + 8, :] = o_ref[0, n : n + 8, :]
        far_ref[0, n : n + 8, :] = o_ref[1, n : n + 8, :]
        for s in range(2):
            swap_ref[s, n : n + 8, :] = o_ref[2 + s, n : n + 8, :]


class Two(tuple):
    def __add__(self, other):
        return Two((self[0] + other[0], self[1] + other[1]))


def sum_rows(row_of):
    core = row_of(7) + row_of(8) + row_of(9) + row_of(10)
    down = [None] * 8
    down[7] = core
    for r in range(6, -1, -1):
        down[r] = down[r + 1] + row_of(r)
    sums = [down[0]]
    up = None
    for r in range(1, 8):
        row = row_of(r + 10)
        up = row if up is None else up + row
        sums.append(down[r] + up)
    return sums


def split(a, b):
    both = jnp.concatenate([a, b], axis=0)
    high = both.astype(jnp.bfloat16)
    low = (both - high.astype(jnp.float32)).astype(jnp.bfloat16)
    return high, low


def twice(tile, sub):
    turned = pltpu.roll(tile, 7, 0)
    return jnp.where(sub == 7, turned, tile), turned


def fill_band(band):
    for block in range(6):
        src = lax.broadcasted_iota(jnp.int32, (LANES, 256), 0)
        dst = lanes_of((LANES, 256))
        if block < 4:
            hit = jnp.abs(src + (block % 2) * LANES - dst) <= HALF_RG
        else:
            x = src % BLOCK
            col = jnp.where(x < HALF_RG, x - HALF_RG, x - HALF_RG + 256)
            hit = (jnp.abs(col - dst) <= HALF_RG) & (x < 2 * HALF_RG)
        band[block * LANES : (block + 1) * LANES, :] = jnp.where(hit, 1.0, 0.0).astype(jnp.bfloat16)


def slot_of(part, q, half):
    return ((part * 2 + q) * 2 + half) * TALL


def prepare(refs, rows, first, dates, halos):
    lane = lanes_of((8, LANES))
    sub = lax.broadcasted_iota(jnp.int32, (8, LANES), 0)
    for row in range(rows):
        for part in range(2):
            base = (row * 2 + part) * 16
            lines = [[None, None] for _ in range(2)]
            for half in range(2):
                for q in range(2):
                    tile = refs[0][q, base + half * 8 : base + half * 8 + 8, :]
                    for ref in refs[1:]:
                        tile = tile + ref[q, base + half * 8 : base + half * 8 + 8, :]
                    slot = slot_of(part, q, half) + first + row
                    dates[slot, 0:8, :], dates[slot, 8:16, :] = twice(tile, sub)
                    lines[q][half] = jnp.broadcast_to(tile[7:8], (8, LANES))
            lines = [jnp.where(sub < 4, low, high) for low, high in lines]
            by_parity = [
                jnp.where(sub % 2 == 0, lines[0], lines[1]),
                jnp.where(sub % 2 == 0, lines[1], lines[0]),
            ]
            halo = by_parity[0]
            halo = jnp.where(lane // BLOCK == sub % 4, halo, 0.0)
            for e in range(1, 4):
                moved = pltpu.roll(by_parity[e % 2], BLOCK * e, 1)
                halo = jnp.where(lane // BLOCK == (sub + e) % 4, moved, halo)
            for at, tile in zip((0, 8), twice(halo, sub)):
                halos[part * TALL + first + row, at : at + 8, :] = tile


def prepare_all(mid, even, odd, dates, halos):
    upper = lax.axis_index("space") % 2 == 0
    prepare([mid], ROWS, HALF_AZ, dates, halos)
    prepare([even], HALF_AZ, jnp.where(upper, HALF_AZ + ROWS, 0), dates, halos)
    prepare(odd, HALF_AZ, jnp.where(upper, 0, HALF_AZ + ROWS), dates, halos)


def put(lhs, rows, tile, sums):
    for r in range(0, 8, 2):
        high, low = split(sums[r], sums[r + 1])
        lhs[rows + r * 8 : rows + r * 8 + 16, tile * LANES : (tile + 1) * LANES] = high
        lhs[rows + r * 8 : rows + r * 8 + 16, (tile + 2) * LANES : (tile + 3) * LANES] = low


def put_halo(lhs, first, step, sums, count=4):
    blocks = lanes_of((16, LANES)) // BLOCK
    keep = [jnp.where(blocks == q, 1.0, 0.0).astype(jnp.bfloat16) for q in range(count)]
    for r in range(0, 8, 2):
        high, low = split(sums[r], sums[r + 1])
        for q in range(count):
            rows = first + q * step + r * 8
            lhs[rows : rows + 16, 4 * LANES : 5 * LANES] = high * keep[q]
            lhs[rows : rows + 16, 5 * LANES : 6 * LANES] = low * keep[q]


def weigh(dates, halos, band, lhs, weights):
    sub = lax.broadcasted_iota(jnp.int32, (8, LANES), 0)

    def energy(ref, re_slot, im_slot):
        def row_of(row):
            re = ref[re_slot + row, 0:8, :]
            im = ref[im_slot + row, 0:8, :]
            return re * re + im * im

        return sum_rows(row_of)

    for q in range(2):
        for half in range(2):
            put(lhs, q * 64, half, energy(dates, slot_of(0, q, half), slot_of(1, q, half)))
    put_halo(lhs, 0, 64, energy(halos, 0, TALL), 2)
    power = jnp.dot(lhs[0:128, :], band[...], preferred_element_type=jnp.float32)
    root = lax.rsqrt(power)
    for q in range(2):
        for r in range(8):
            for half in range(2):
                tile = root[q * 64 + r * 8 : q * 64 + r * 8 + 8, half * LANES : (half + 1) * LANES]
                slot = (q * 8 + r) * 2 + half
                weights[slot, 0:8, :], weights[slot, 8:16, :] = twice(tile, sub)


def cross_rows(load_i, load_j):
    def row_of(row):
        (are, aim), (bre, bim) = load_i(row), load_j(row)
        return Two((are * bre + aim * bim, aim * bre - are * bim))

    return sum_rows(row_of)


def main_tile(ref, q, half, m):
    re, im = slot_of(0, q, half), slot_of(1, q, half)
    return lambda row: (ref[re + row, pl.ds(m, 8), :], ref[im + row, pl.ds(m, 8), :])


def build_main(lhs, at, left, right, m):
    for half in range(2):
        sums = cross_rows(main_tile(*left, half, 0), main_tile(*right, half, m))
        put(lhs, at, half, [s[0] for s in sums])
        put(lhs, at + 64, half, [s[1] for s in sums])


def build_halo(lhs, load_i, load_j, count=4):
    sums = cross_rows(load_i, load_j)
    put_halo(lhs, 0, 128, [s[0] for s in sums], count)
    put_halo(lhs, 64, 128, [s[1] for s in sums], count)


def finish(lhs, band, weigh_of, res, base, count=4):
    boxed = jnp.dot(lhs[0 : count * 128, :], band[...], preferred_element_type=jnp.float32)
    for q in range(count):
        (wi_ref, wi_q), (wj_ref, wj_q), m = weigh_of(q)
        for r in range(8):
            for half in range(2):
                cols = slice(half * LANES, (half + 1) * LANES)
                re = boxed[q * 128 + r * 8 : q * 128 + r * 8 + 8, cols]
                im = boxed[q * 128 + 64 + r * 8 : q * 128 + 64 + r * 8 + 8, cols]
                square = re * re + im * im
                size = square * lax.rsqrt(jnp.maximum(square, TINY))
                wi = wi_ref[(wi_q * 8 + r) * 2 + half, 0:8, :]
                wj = wj_ref[(wj_q * 8 + r) * 2 + half, pl.ds(m, 8), :]
                start = pl.multiple_of(base + q * 128 + half * 64 + r * 8, 8)
                res[pl.ds(start, 8), :] = size * wi * wj


def inner_unit(n, dates, halos):
    lane = lanes_of((8, LANES))
    pair = INNER[2 * n : 2 * n + 2]

    def build(lhs):
        for s, (same, m) in enumerate(pair):
            for q in range(2):
                other = q if same else 1 - q
                build_main(lhs, (s * 2 + q) * 128, (dates, q), (dates, other), m)

        def load_i(row):
            return halos[row, 0:8, :], halos[TALL + row, 0:8, :]

        def load_j(row):
            out = []
            for part in range(2):
                tiles = []
                for same, m in pair:
                    tile = halos[part * TALL + row, pl.ds(m, 8), :]
                    tiles.append(tile if same else pltpu.roll(tile, BLOCK, 1))
                out.append(jnp.where(lane < 2 * BLOCK, tiles[0], tiles[-1]) if len(tiles) > 1 else tiles[0])
            return out

        build_halo(lhs, load_i, load_j, 2 * len(pair))

    def weigh_of(weights):
        def of(q):
            same, m = pair[q // 2]
            return (weights, q % 2), (weights, q % 2 if same else 1 - q % 2), m

        return of

    return build, weigh_of


def near_kernel(mid, even, odd, dates, halos, weights, band, res, lhs_a, lhs_b):
    fill_band(band)
    prepare_all(mid, even, [odd], dates, halos)
    weigh(dates, halos, band, lhs_b, weights)
    units = [inner_unit(n, dates, halos) for n in range(4)]
    buffers = [lhs_a, lhs_b]
    units[0][0](buffers[0])
    for n in range(4):
        if n < 3:
            units[n + 1][0](buffers[(n + 1) % 2])
        finish(buffers[n % 2], band, units[n][1](weights), res, n * 512, min(4, 2 * (len(INNER) - 2 * n)))


def far_kernel(
    table, mid, even, odd, odd_far, dates_n, halos_n, weights_n, band, res_n, o_ref,
    dates_f, halos_f, halos_o, weights_f, lhs_a, lhs_b, res, out, sems,
):
    lane = lanes_of((8, LANES))
    prepare_all(mid, even, [odd, odd_far], dates_f, halos_f)
    weigh(dates_f, halos_f, band, lhs_b, weights_f)
    for n in range(0, NEAR_ROWS, 8):
        res[n : n + 8, :] = res_n[n : n + 8, :]

    units = [inner_unit(n, dates_f, halos_f) for n in range(4)]
    sides_d = [(dates_n, 0), (dates_n, 1), (dates_f, 0), (dates_f, 1)]
    sides_w = [(weights_n, 0), (weights_n, 1), (weights_f, 0), (weights_f, 1)]

    for part in range(2):
        for row in range(TALL):
            slot = part * TALL + row
            for at in (0, 8):
                near = halos_n[slot, at : at + 8, :]
                far = halos_f[slot, at : at + 8, :]
                if at == 0:
                    halos_o[slot, 0:8, :] = jnp.where(lane < 2 * BLOCK, near, far)
                near = pltpu.roll(near, BLOCK, 1)
                halos_o[2 * TALL + slot, at : at + 8, :] = jnp.where(lane < 2 * BLOCK, far, near)

    def outer_build(m, lhs):
        for q, (pi, pj) in enumerate(OUTER):
            build_main(lhs, q * 128, sides_d[pi], sides_d[pj], m)
        build_halo(
            lhs,
            lambda row: (halos_o[row, 0:8, :], halos_o[TALL + row, 0:8, :]),
            lambda row: (
                halos_o[2 * TALL + row, pl.ds(m, 8), :],
                halos_o[3 * TALL + row, pl.ds(m, 8), :],
            ),
        )

    def outer_finish(m, lhs):
        def of(q):
            pi, pj = OUTER[q]
            return sides_w[pi], sides_w[pj], m

        finish(lhs, band, of, res, 2 * NEAR_ROWS + m * 512)

    buffers = [lhs_a, lhs_b]
    units[0][0](buffers[0])
    for n in range(4):
        if n < 3:
            units[n + 1][0](buffers[(n + 1) % 2])
        else:
            outer_build(0, lhs_a)
        finish(buffers[n % 2], band, units[n][1](weights_f), res, NEAR_ROWS + n * 512, min(4, 2 * (len(INNER) - 2 * n)))

    for m in range(7):
        if m < 6:
            outer_build(m + 1, buffers[(m + 1) % 2])
        outer_finish(m, buffers[m % 2])

    mine = lax.axis_index("date") * (LAGS * DATES)
    size = DATES * 16

    def copy_of(k):
        rows = pl.ds(pl.multiple_of(k * size, size), size)
        return pltpu.make_async_copy(out.at[rows], o_ref.at[rows], sems.at[k])

    def emit(k, carry):
        for i in range(DATES):
            start = table[mine + k * DATES + i]
            for half in range(2):
                target = pl.multiple_of(k * size + i * 16 + half * 8, 8)
                out[pl.ds(target, 8), :] = res[pl.ds(start + half * 64, 8, stride=8), :]
        copy_of(k).start()
        return carry

    lax.fori_loop(0, LAGS, emit, 0)

    def settle(k, carry):
        copy_of(k).wait()
        return carry

    lax.fori_loop(0, LAGS, settle, 0)


VMEM = pl.BlockSpec(memory_space=pltpu.VMEM)
DATES_SHAPE = (2 * 2 * 2 * TALL, 16, LANES)
HALOS_SHAPE = (2 * TALL, 16, LANES)
WEIGHTS_SHAPE = (2 * 8 * 2, 16, LANES)
BAND_SHAPE = (6 * LANES, 256)
LHS_SHAPE = (512, 6 * LANES)


def pack(stack):
    flat = stack.reshape(2, PER, ROWS, TILES, LANES).transpose(0, 1, 3, 2, 4).reshape(-1, LANES)
    return pl.pallas_call(
        pack_kernel,
        out_shape=[jax.ShapeDtypeStruct((n, MIDLEN, LANES), jnp.float32) for n in (1, 1, 2)],
        in_specs=[VMEM],
        out_specs=[VMEM] * 3,
        scratch_shapes=[pltpu.VMEM((GROUPS, MIDLEN, LANES), jnp.float32)],
        compiler_params=pltpu.CompilerParams(vmem_limit_bytes=4 * 1024 * 1024),
        name="pack",
    )(flat)


def near_part(mid, even, odd):
    shapes = [
        (DATES_SHAPE, jnp.float32),
        (HALOS_SHAPE, jnp.float32),
        (WEIGHTS_SHAPE, jnp.float32),
        (BAND_SHAPE, jnp.bfloat16),
        ((NEAR_ROWS, LANES), jnp.float32),
    ]
    return pl.pallas_call(
        near_kernel,
        out_shape=[jax.ShapeDtypeStruct(shape, dtype) for shape, dtype in shapes],
        in_specs=[VMEM] * 3,
        out_specs=[VMEM] * 5,
        scratch_shapes=[pltpu.VMEM(LHS_SHAPE, jnp.bfloat16)] * 2,
        compiler_params=pltpu.CompilerParams(vmem_limit_bytes=16 * 1024 * 1024),
        cost_estimate=pl.CostEstimate(flops=1_600_000_000, bytes_accessed=6_000_000, transcendentals=0),
        name="near",
    )(mid, even, odd)


def far_part(mid, even, odd, odd_far, near):
    out = pl.pallas_call(
        far_kernel,
        out_shape=jax.ShapeDtypeStruct((LAGS * DATES * 2 * 8, LANES), jnp.float32),
        in_specs=[pl.BlockSpec(memory_space=pltpu.SMEM)] + [VMEM] * 9,
        out_specs=pl.BlockSpec(memory_space=pl.ANY),
        scratch_shapes=[
            pltpu.VMEM(DATES_SHAPE, jnp.float32),
            pltpu.VMEM(HALOS_SHAPE, jnp.float32),
            pltpu.VMEM((4 * TALL, 16, LANES), jnp.float32),
            pltpu.VMEM(WEIGHTS_SHAPE, jnp.float32),
            pltpu.VMEM(LHS_SHAPE, jnp.bfloat16),
            pltpu.VMEM(LHS_SHAPE, jnp.bfloat16),
            pltpu.VMEM((RES_ROWS, LANES), jnp.float32),
            pltpu.VMEM((LAGS * DATES * 2 * 8, LANES), jnp.float32),
            pltpu.SemaphoreType.DMA((LAGS,)),
        ],
        compiler_params=pltpu.CompilerParams(vmem_limit_bytes=32 * 1024 * 1024),
        cost_estimate=pl.CostEstimate(flops=4_800_000_000, bytes_accessed=9_000_000, transcendentals=0),
        name="far",
    )(jnp.asarray(lag_tables()), mid, even, odd, odd_far, *near)
    return (
        out.reshape(LAGS, DATES, 2, ROWS, LANES)
        .transpose(0, 1, 3, 2, 4)
        .reshape(LAGS, DATES, ROWS, 2 * LANES)
    )


def body(stack):
    peers = lax.axis_size("space")
    sibling = [(i, i ^ 1) for i in range(GROUPS)]
    across = [(i, i ^ 2) for i in range(GROUPS)]
    even_pairs = [(i, i ^ 1) for i in range(peers)]
    odd_pairs = [(i, i + 1) for i in range(1, peers - 1, 2)]
    odd_pairs += [(j, i) for i, j in odd_pairs]
    flat_pairs = [(i, j) for i, j in odd_pairs if i // PLANE == j // PLANE]
    cross_pairs = [
        (d * peers + i, (d ^ 2) * peers + j)
        for d in range(GROUPS)
        for i, j in odd_pairs
        if i // PLANE != j // PLANE
    ]
    upper = lax.axis_index("space") % 2 == 0

    def edges(mid):
        first, last = mid[:, :HALOLEN], mid[:, MIDLEN - HALOLEN :]
        return jnp.where(upper, first, last), jnp.where(upper, last, first)

    kept, sent, swap = pack(stack)
    swapped = lax.ppermute(swap, "date", sibling)
    away = jnp.concatenate([sent, swapped[1:2]])
    far = lax.ppermute(away, "date", across)
    near = jnp.concatenate([kept, swapped[0:1]])
    near_odd, near_even = edges(near)
    far_cross = lax.ppermute(edges(away)[0], ("date", "space"), cross_pairs)
    near_even = lax.ppermute(near_even, "space", even_pairs)
    near_odd, near_even = lax.optimization_barrier((near_odd, near_even))
    near_odd = lax.ppermute(near_odd, "space", odd_pairs)
    far_odd, far_even = edges(far)
    far_odd = lax.ppermute(far_odd, "space", flat_pairs)
    far_even = lax.ppermute(far_even, "space", even_pairs)
    return far_part(far, far_even, far_odd, far_cross, near_part(near, near_even, near_odd))


def solution(mesh):
    in_specs = (P(None, "date", "space", None),)
    out_specs = P(None, None, "space", "date")
    return jax.shard_map(body, mesh=mesh, in_specs=in_specs, out_specs=out_specs, check_vma=False)
```
